512 devices in a mesh: dp: 16 (over z_lo, x), expert: 32 (over z_hi, y, core).
Axes of the slice: x: 4, y: 8, z: 8 (z_hi: 2, z_lo: 4; z = z_hi * 4 + z_lo), core: 2. Of those that a mesh axis runs over, the one named last changes fastest.
Arguments:
- tokens: bfloat16 [65536, 2048], P(('dp', 'expert')), parts along dimension 0, may hold values from -6 to 6
- routes: int32 [65536, 2], P(('dp', 'expert')), parts along dimension 0, may hold values from 0 to 7, all different within a row; in each aligned block of 128 rows (0 to 127, 128 to 255, ...) at most 48 rows name the same one
- gates: float32 [65536, 2], P(('dp', 'expert')), parts along dimension 0, may hold values from 0.25 to 1
- hot_ids: int32 [32], P('dp'), parts along dimension 0, may hold values from 0 to 7, as said below
- capacity: int32 [128], P('dp'), parts along dimension 0, may hold values from 1 to 48, as said below
- gate_up: bfloat16 [2, 2048, 8192], P(None, None, 'expert'), may hold values from -0.125 to 0.125
- down: bfloat16 [8192, 2048], P('expert'), may hold values from -0.1875 to 0.1875
Outputs:
- mixed: bfloat16 [65536, 2048], P(('dp', 'expert')), parts along dimension 0
The draws below stay inside these ranges and needn't reach their ends.
There are 16 independent parts, one for each index of `dp`. The reference program is written for one: setup_inputs(seed, part) draws one part's arguments, and reference() takes and returns one part's arrays. A program takes and returns all parts, laid end to end along the dimension named above; an argument that names none is the same for every part. Nothing has to cross between parts.
Inputs may be any that keep to these rules, and one draw needn't show every extreme that they name: `routes`: each row names 2 different experts; among the rows of one device no expert is named more than 48 times. `hot_ids`: 2 different experts. `capacity`: some entry equals 48.
All inputs are finite; a program needn't handle non-finite values.
Results may differ from the reference program's by a relative error of at most 0.0057.
Values may be sent and summed in bfloat16 or wider, within the bound.
No kernel may reach another device: no remote copies, remote signals or barrier semaphores. Data moves between devices by JAX's collectives and lax.ppermute only.
A program may use at most 64 MiB of HBM per device.

```python
import math
import jax
import jax.numpy as jnp
import numpy as np
from jax import lax

D = 2048
FF = 1024
EXPERTS = 8
TOP = 2
HOT = 2
TOK_DEV = 128
CAP = 48
TOKENS = 4096
N_EXPERT = 32


def draw_hot_ids(key, part):
    order = jax.random.permutation(jax.random.fold_in(key, 11), EXPERTS)
    return order[:HOT].astype(jnp.int32)


def draw_capacity(key, part):
    first_key = jax.random.fold_in(key, 23)
    second_key = jax.random.fold_in(key, 29)
    values = jax.random.randint(first_key, (EXPERTS,), 1, CAP + 1)
    place = jax.random.randint(second_key, (), 0, EXPERTS)
    return jnp.where(jnp.arange(EXPERTS) == place, CAP, values).astype(jnp.int32)


def block_scale(own_key, extent, shards, least, largest):
    def one(dim, shards_of):
        steps = jax.random.uniform(jax.random.fold_in(jax.random.fold_in(own_key, 6), dim), (shards_of,), jnp.float32, least / len(shards), largest / len(shards))
        return jnp.repeat(jnp.exp(steps), extent[dim] // shards_of).reshape((-1,) + (1,) * (len(extent) - dim - 1))

    gain = one(*shards[0])
    for cut in shards[1:]:
        gain = gain * one(*cut)
    return gain


def shared_out(own_key, own, number, rows, number_of, top, most, slope):
    ranking = jax.random.permutation(own_key, number_of)
    packed, common = load_shares(number_of, rows * top, most, slope, True), load_shares(number_of, rows * top, most, slope, False)
    places = jnp.arange(number_of)

    def named(sizes, rotation):
        used = int((sizes > 0).sum())
        fixed = max(1, used // 4)
        shifted = fixed + (places - fixed + rotation * (used - fixed)) % max(1, number_of - fixed)
        return jnp.zeros((number_of,), jnp.int32).at[ranking[jnp.where(places < fixed, places, shifted)]].set(jnp.asarray(sizes, jnp.int32))

    sizes = jnp.where(number % 4 == 0, named(packed, number // 4), named(common, number - number // 4 - 1))
    mixed = jax.random.permutation(jax.random.fold_in(own, 3), number_of)
    source_of, taker = mixed[0:number_of // 2 * 2:2], mixed[1:number_of // 2 * 2:2]
    margin = jnp.minimum(sizes[source_of] - 1, most - sizes[taker]) // 2
    margin = jnp.where((source_of == ranking[0]) | (taker == ranking[0]) | (sizes[taker] == 0), 0, jnp.maximum(margin, 0))
    shifted = jax.random.randint(jax.random.fold_in(own, 4), (number_of // 2,), 0, 1 << 20) % (margin + 1)
    sizes = sizes.at[source_of].add(-shifted).at[taker].add(shifted)
    items = jnp.searchsorted(jnp.cumsum(sizes), jnp.arange(rows * top), side="right").astype(jnp.int32)
    table = items.reshape(top, rows).T
    table = table[jax.random.permutation(jax.random.fold_in(own, 1), rows)]
    rotation = jax.random.randint(jax.random.fold_in(own, 2), (rows, 1), 0, top)
    return jnp.take_along_axis(table, (jnp.arange(top)[None, :] + rotation) % top, axis=1)


def load_shares(amount, total, most, skew, full):
    portions = [(1 << 20) // math.isqrt(grade ** skew) + 1 for grade in range(1, amount + 1)]
    largest = most if full else min(most, max(-(-total // amount), total * portions[0] // sum(portions)))
    least = 1 if total - largest >= amount - 1 else 0
    counts, spare = [largest] + [least] * (amount - 1), total - largest - least * (amount - 1)
    while spare > 0:
        free = [i for i in range(1, amount) if counts[i] < largest] or [i for i in range(1, amount) if counts[i] < most]
        whole, budget = sum([portions[i] for i in free]), spare
        for i in free:
            more = min(most - counts[i], max(1, budget * portions[i] // whole), spare)
            counts[i] = counts[i] + more
            spare = spare - more
    return np.array(counts)


def normal_values(own_key, extent, deviation, reach, shards=(), kind=jnp.bfloat16):
    gain = block_scale(own_key, extent, shards, -0.22, 0.18) if shards else 1.0
    entries = jax.random.normal(own_key, extent, jnp.float32) * deviation * gain
    return jnp.minimum(jnp.maximum(entries, -reach), reach).astype(kind)


def setup_inputs(seed: int = 0, part: int = 0) -> dict:
    seeds = jax.random.split(jax.random.key(seed), 8)
    part_splits = jax.random.split(jax.random.fold_in(seeds[7], part), 8)
    tokens = normal_values(part_splits[0], (TOKENS, D), 1.0, 6.0, ((0, 32),))
    routes_keys = jax.random.split(jax.random.fold_in(part_splits[1], 1), TOKENS // TOK_DEV)
    routes_turns = jax.random.permutation(jax.random.fold_in(part_splits[1], 3), TOKENS // TOK_DEV)
    routes = jax.vmap(lambda own, number: shared_out(jax.random.fold_in(part_splits[1], 2), own, number, TOK_DEV, EXPERTS, TOP, CAP, 2))(routes_keys, routes_turns).reshape((TOKENS, TOP))
    gates = jnp.clip(0.25 + 0.75 * jax.random.uniform(part_splits[2], (TOKENS, TOP), jnp.float32) ** block_scale(part_splits[2], (TOKENS, TOP), ((0, 32),), -0.2, 0.2), 0.25, 1.0)
    hot_ids = draw_hot_ids(jax.random.fold_in(jax.random.fold_in(seeds[7], part), 71), part)
    capacity = draw_capacity(jax.random.fold_in(jax.random.fold_in(seeds[7], part), 71), part)
    gate_up = normal_values(seeds[5], (2, D, EXPERTS * FF), D ** -0.5, 0.125, ((2, 32),))
    down = normal_values(seeds[6], (EXPERTS * FF, D), FF ** -0.5, 0.1875, ((0, 32),))
    return dict(tokens=tokens, routes=routes, gates=gates, hot_ids=hot_ids, capacity=capacity, gate_up=gate_up, down=down)


def kept_routes(routes, hot_ids, capacity):
    flat = routes.reshape(N_EXPERT, TOK_DEV * TOP)
    one_hot = (flat[:, :, None] == jnp.arange(EXPERTS, dtype=jnp.int32)[None, None, :]).astype(jnp.int32)
    before = jnp.cumsum(one_hot, axis=1) - one_hot
    position = jnp.sum(before * one_hot, axis=2)
    is_hot = jnp.any(jnp.arange(EXPERTS, dtype=jnp.int32)[:, None] == hot_ids[None, :], axis=1)
    limits = jnp.where(is_hot, jnp.full((EXPERTS,), CAP, jnp.int32), capacity)
    route_limit = jnp.sum(one_hot * limits[None, None, :], axis=2)
    return (position < route_limit).reshape(routes.shape)


def reference(tokens, routes, gates, hot_ids, capacity, gate_up, down):
    group_size = N_EXPERT // EXPERTS
    hid_width = FF // group_size
    feat_width = tokens.shape[1]
    limit = CAP * N_EXPERT
    keep = kept_routes(routes, hot_ids, capacity)

    def add_expert(total, expert_id):
        chosen = jnp.logical_and(routes == expert_id, keep)
        weight_row = jnp.sum(jnp.where(chosen, gates, jnp.zeros_like(gates)), axis=1)
        is_routed = jnp.any(chosen, axis=1)
        index_list = jnp.nonzero(is_routed, size=limit, fill_value=0)[0].astype(jnp.int32)
        is_valid = jnp.arange(limit, dtype=jnp.int32) < jnp.sum(is_routed.astype(jnp.int32))
        row_block = tokens[index_list]
        start = (expert_id * FF).astype(jnp.int32)
        w_gate = lax.dynamic_slice_in_dim(gate_up[0], start, FF, 1)
        w_up = lax.dynamic_slice_in_dim(gate_up[1], start, FF, 1)
        w_down = lax.dynamic_slice_in_dim(down, start, FF, 0)
        gate_act = jnp.dot(row_block, w_gate, preferred_element_type=jnp.float32)
        up_act = jnp.dot(row_block, w_up, preferred_element_type=jnp.float32)
        hidden = (jax.nn.silu(gate_act) * up_act).astype(jnp.bfloat16)
        summed = jnp.zeros((limit, feat_width), jnp.float32)
        for slot_index in range(group_size):
            lower = slot_index * hid_width
            term = jnp.dot(hidden[:, lower:lower + hid_width], w_down[lower:lower + hid_width, :],
                           preferred_element_type=jnp.float32).astype(jnp.bfloat16)
            term = lax.optimization_barrier(term)
            summed = summed + term.astype(jnp.float32)
        scale = jnp.where(is_valid, weight_row[index_list], jnp.zeros_like(weight_row[index_list]))
        total = total.at[index_list].add(summed * scale[:, None])
        return total, None

    start_total = jnp.zeros((tokens.shape[0], feat_width), jnp.float32)
    total = lax.scan(add_expert, start_total, jnp.arange(EXPERTS, dtype=jnp.int32))[0]
    return total.astype(jnp.bfloat16)
```

```python
import jax
import jax.numpy as jnp
from jax import lax
from jax.experimental import pallas as pl
from jax.experimental.pallas import tpu as pltpu
from jax.sharding import Mesh, PartitionSpec as P

EXPERTS = 8
CAP = 48
F32 = jnp.float32
BF16 = jnp.bfloat16
AXES = ("zl", "x", "zh", "yp", "yq", "core")
SIZES = (4, 4, 2, 4, 2, 2)
VMEM = pl.BlockSpec(memory_space=pltpu.VMEM)
SMEM = pl.BlockSpec(memory_space=pltpu.SMEM)
HBM = pl.BlockSpec(memory_space=pl.ANY)
PIECES = 4
VMEM_LIMIT = 32 << 20


def swap(value, axis):
    return lax.ppermute(value, axis, [(0, 1), (1, 0)])


def limits_of(hot_ids, capacity):
    e = jnp.arange(EXPERTS, dtype=jnp.int32)
    hot = jnp.logical_or(e == hot_ids[0], e == hot_ids[1])
    return jnp.where(hot, CAP, capacity)


def chosen_rows(limits_ref, routes_ref):
    rows = EXPERTS * CAP
    tokens = routes_ref.shape[1]
    row = lax.broadcasted_iota(jnp.int32, (rows, 1), 0)
    expert = lax.div(row, CAP)
    limit = jnp.zeros((rows, 1), jnp.int32)
    for j in range(EXPERTS):
        limit = jnp.where(expert == j, limits_ref[j], limit)
    first = routes_ref[0:1, :] == expert
    second = routes_ref[1:2, :] == expert
    named = jnp.logical_or(first, second)
    earlier = lax.broadcasted_iota(jnp.int32, (tokens, tokens), 0) < lax.broadcasted_iota(
        jnp.int32, (tokens, tokens), 1
    )
    rank = jnp.dot(
        jnp.where(named, 1.0, 0.0).astype(BF16),
        jnp.where(earlier, 1.0, 0.0).astype(BF16),
        preferred_element_type=F32,
    ).astype(jnp.int32)
    kept = jnp.logical_and(named, rank < limit)
    return jnp.logical_and(kept, rank == lax.rem(row, CAP)), first


def pack_kernel(limits_ref, routes_ref, tokens_ref, packed_ref):
    chosen, _ = chosen_rows(limits_ref, routes_ref)
    place = jnp.where(chosen, 1.0, 0.0).astype(BF16)
    packed_ref[...] = jnp.dot(place, tokens_ref[...], preferred_element_type=F32).astype(BF16)


def pack(limits, routes, tokens):
    count, width = tokens.shape
    return pl.pallas_call(
        pack_kernel,
        out_shape=jax.ShapeDtypeStruct((EXPERTS * CAP, width), BF16),
        in_specs=[SMEM, VMEM, VMEM],
        out_specs=VMEM,
        cost_estimate=pl.CostEstimate(
            flops=2 * EXPERTS * CAP * count * width, bytes_accessed=2 * (EXPERTS * CAP + count) * width, transcendentals=0
        ),
        compiler_params=pltpu.CompilerParams(vmem_limit_bytes=VMEM_LIMIT),
    )(limits, routes, tokens)


def weights_kernel(limits_ref, routes_ref, gates_ref, hi_ref, lo_ref):
    chosen, first = chosen_rows(limits_ref, routes_ref)
    weight = jnp.where(first, gates_ref[0:1, :], gates_ref[1:2, :])
    weight = jnp.where(chosen, weight, 0.0).T
    hi = weight.astype(BF16)
    hi_ref[...] = hi
    lo_ref[...] = (weight - hi.astype(F32)).astype(BF16)


def row_weights(limits, routes, gates):
    shape = jax.ShapeDtypeStruct((routes.shape[1], EXPERTS * CAP), BF16)
    return pl.pallas_call(
        weights_kernel,
        out_shape=[shape, shape],
        in_specs=[SMEM, VMEM, VMEM],
        out_specs=[VMEM, VMEM],
        cost_estimate=pl.CostEstimate(flops=2 * 384 * 128 * 128, bytes_accessed=400000, transcendentals=0),
        compiler_params=pltpu.CompilerParams(vmem_limit_bytes=VMEM_LIMIT),
    )(limits, routes, gates)


def combine_kernel(hi_ref, lo_ref, rows_ref, out_ref):
    rows = rows_ref[...]
    total = jnp.dot(hi_ref[...], rows, preferred_element_type=F32)
    total += jnp.dot(lo_ref[...], rows, preferred_element_type=F32)
    out_ref[...] = total.astype(BF16)


def combine(hi, lo, rows):
    count, width = hi.shape[0], rows.shape[1]
    return pl.pallas_call(
        combine_kernel,
        out_shape=jax.ShapeDtypeStruct((count, width), BF16),
        in_specs=[VMEM] * 3,
        out_specs=VMEM,
        cost_estimate=pl.CostEstimate(
            flops=4 * EXPERTS * CAP * count * width, bytes_accessed=2 * (EXPERTS * CAP + count) * width, transcendentals=0
        ),
        compiler_params=pltpu.CompilerParams(vmem_limit_bytes=VMEM_LIMIT),
    )(hi, lo, rows)


def piece_kernel(at_ref, gate_up_ref, down_ref, out_ref):
    half = down_ref.shape[0]
    out_ref[0:2] = gate_up_ref[...]
    for i in range(2):
        out_ref[2, i * half : (i + 1) * half] = down_ref[:, i * half : (i + 1) * half]


def piece(at, gate_up, down):
    _, width, hidden = gate_up.shape
    rows = width // PIECES
    return pl.pallas_call(
        piece_kernel,
        out_shape=jax.ShapeDtypeStruct((3, rows, hidden), BF16),
        grid_spec=pltpu.PrefetchScalarGridSpec(
            num_scalar_prefetch=1,
            grid=(1,),
            in_specs=[
                pl.BlockSpec((2, rows, hidden), lambda i, at: (0, at[0], 0)),
                pl.BlockSpec((hidden, rows), lambda i, at: (0, at[0])),
            ],
            out_specs=pl.BlockSpec((3, rows, hidden), lambda i, at: (0, 0, 0)),
        ),
        cost_estimate=pl.CostEstimate(flops=0, bytes_accessed=12 * rows * hidden, transcendentals=0),
        compiler_params=pltpu.CompilerParams(vmem_limit_bytes=VMEM_LIMIT),
    )(at, gate_up, down)


def silu_up(gate, up):
    return (gate / (1.0 + jnp.exp(-gate)) * up).astype(BF16)


def experts_kernel(rows_ref, *refs):
    whole, (other_ref, out_ref, total_ref) = refs[:4], refs[4:]
    for s in range(2):
        gate_up_ref, down_ref = whole[2 * s], whole[2 * s + 1]
        rows = rows_ref[...]
        gate = jnp.dot(rows, gate_up_ref[0], preferred_element_type=F32)
        up = jnp.dot(rows, gate_up_ref[1], preferred_element_type=F32)
        term = jnp.dot(silu_up(gate, up), down_ref[...], preferred_element_type=F32)
        if s == 0:
            total_ref[...] = term
        else:
            total_ref[...] += term
    size = other_ref.shape[2]
    for s in range(2):
        half = size // 2
        gate = up = None
        for k in range(PIECES):
            rows = rows_ref[:, k * size : (k + 1) * size]
            g = jnp.dot(rows, other_ref[2 * k + s, 0], preferred_element_type=F32)
            u = jnp.dot(rows, other_ref[2 * k + s, 1], preferred_element_type=F32)
            gate, up = (g, u) if gate is None else (gate + g, up + u)
        hidden = silu_up(gate, up)
        for k in range(PIECES):
            for n in range(2):
                at = slice(k * size + n * half, k * size + (n + 1) * half)
                tile = other_ref[2 * k + s, 2, n * half : (n + 1) * half]
                term = total_ref[:, at] + jnp.dot(hidden, tile, preferred_element_type=F32)
                if s == 0:
                    total_ref[:, at] = term
                else:
                    out_ref[:, at] = term.astype(BF16)


def experts(rows, whole, other):
    count, width = rows.shape
    hidden = whole[0].shape[2]
    return pl.pallas_call(
        experts_kernel,
        out_shape=jax.ShapeDtypeStruct((count, width), BF16),
        in_specs=[VMEM] * 6,
        out_specs=VMEM,
        scratch_shapes=[pltpu.VMEM((count, width), F32)],
        cost_estimate=pl.CostEstimate(
            flops=24 * count * width * hidden, bytes_accessed=24 * width * hidden, transcendentals=4 * count * hidden
        ),
        compiler_params=pltpu.CompilerParams(vmem_limit_bytes=VMEM_LIMIT),
    )(rows, *whole, other)


def exchange(rows):
    width = rows.shape[1]
    blocks = rows.reshape(EXPERTS, CAP, width)
    return lax.all_to_all(blocks, ("zh", "yp"), 0, 0, tiled=True).reshape(EXPERTS * CAP, width)


def local(tokens, routes, gates, hot_ids, capacity, gate_up, down):
    x = lax.axis_index("x").astype(jnp.int32).reshape(1)
    near = swap(piece(x, gate_up, down), "yq")
    limits = limits_of(hot_ids, capacity)
    packed = pack(limits, routes.T, tokens)
    hi, lo = row_weights(limits, routes.T, gates.T)
    near, packed = lax.optimization_barrier((near, packed))
    arrived = exchange(packed)
    other = lax.all_gather(near, ("x", "core"), axis=0, tiled=False)
    whole = (gate_up, down, swap(gate_up, "core"), swap(down, "core"))
    back = exchange(experts(arrived, whole, other))
    return combine(hi, lo, back)


def solution(mesh):
    fine = Mesh(mesh.devices.reshape(SIZES), AXES)
    dp, expert = AXES[:2], AXES[2:]
    in_specs = (
        P(AXES, None),
        P(AXES, None),
        P(AXES, None),
        P(dp),
        P(dp),
        P(None, None, expert),
        P(expert, None),
    )
    return jax.shard_map(local, mesh=fine, in_specs=in_specs, out_specs=P(AXES, None), check_vma=False)
```

```python
import jax
import jax.numpy as jnp
from jax import lax
from jax.experimental import pallas as pl
from jax.experimental.pallas import tpu as pltpu
from jax.sharding import Mesh, PartitionSpec as P

EXPERTS = 8
CAP = 48
F32 = jnp.float32
BF16 = jnp.bfloat16
AXES = ("zl", "x", "zh", "yp", "yq", "core")
SIZES = (4, 4, 2, 4, 2, 2)
VMEM = pl.BlockSpec(memory_space=pltpu.VMEM)
SMEM = pl.BlockSpec(memory_space=pltpu.SMEM)
HBM = pl.BlockSpec(memory_space=pl.ANY)
PIECES = 4
STEPS = (0, 3, 1, 2)
VMEM_LIMIT = 32 << 20


def swap(value, axis):
    return lax.ppermute(value, axis, [(0, 1), (1, 0)])


def shift(value, by):
    return lax.ppermute(value, "x", [(i, (i + by) % 4) for i in range(4)])


def limits_of(hot_ids, capacity):
    e = jnp.arange(EXPERTS, dtype=jnp.int32)
    hot = jnp.logical_or(e == hot_ids[0], e == hot_ids[1])
    return jnp.where(hot, CAP, capacity)


def chosen_rows(limits_ref, routes_ref):
    rows = EXPERTS * CAP
    tokens = routes_ref.shape[1]
    row = lax.broadcasted_iota(jnp.int32, (rows, 1), 0)
    expert = lax.div(row, CAP)
    limit = jnp.zeros((rows, 1), jnp.int32)
    for j in range(EXPERTS):
        limit = jnp.where(expert == j, limits_ref[j], limit)
    first = routes_ref[0:1, :] == expert
    second = routes_ref[1:2, :] == expert
    named = jnp.logical_or(first, second)
    earlier = lax.broadcasted_iota(jnp.int32, (tokens, tokens), 0) < lax.broadcasted_iota(
        jnp.int32, (tokens, tokens), 1
    )
    rank = jnp.dot(
        jnp.where(named, 1.0, 0.0).astype(BF16),
        jnp.where(earlier, 1.0, 0.0).astype(BF16),
        preferred_element_type=F32,
    ).astype(jnp.int32)
    kept = jnp.logical_and(named, rank < limit)
    return jnp.logical_and(kept, rank == lax.rem(row, CAP)), first


def pack_kernel(limits_ref, routes_ref, tokens_ref, packed_ref):
    chosen, _ = chosen_rows(limits_ref, routes_ref)
    place = jnp.where(chosen, 1.0, 0.0).astype(BF16)
    packed_ref[...] = jnp.dot(place, tokens_ref[...], preferred_element_type=F32).astype(BF16)


def pack(limits, routes, tokens):
    count, width = tokens.shape
    return pl.pallas_call(
        pack_kernel,
        out_shape=jax.ShapeDtypeStruct((EXPERTS * CAP, width), BF16),
        in_specs=[SMEM, VMEM, VMEM],
        out_specs=VMEM,
        cost_estimate=pl.CostEstimate(
            flops=2 * EXPERTS * CAP * count * width, bytes_accessed=2 * (EXPERTS * CAP + count) * width, transcendentals=0
        ),
        compiler_params=pltpu.CompilerParams(vmem_limit_bytes=VMEM_LIMIT),
    )(limits, routes, tokens)


def weights_kernel(limits_ref, routes_ref, gates_ref, hi_ref, lo_ref):
    chosen, first = chosen_rows(limits_ref, routes_ref)
    weight = jnp.where(first, gates_ref[0:1, :], gates_ref[1:2, :])
    weight = jnp.where(chosen, weight, 0.0).T
    hi = weight.astype(BF16)
    hi_ref[...] = hi
    lo_ref[...] = (weight - hi.astype(F32)).astype(BF16)


def row_weights(limits, routes, gates):
    shape = jax.ShapeDtypeStruct((routes.shape[1], EXPERTS * CAP), BF16)
    return pl.pallas_call(
        weights_kernel,
        out_shape=[shape, shape],
        in_specs=[SMEM, VMEM, VMEM],
        out_specs=[VMEM, VMEM],
        cost_estimate=pl.CostEstimate(flops=2 * 384 * 128 * 128, bytes_accessed=400000, transcendentals=0),
        compiler_params=pltpu.CompilerParams(vmem_limit_bytes=VMEM_LIMIT),
    )(limits, routes, gates)


def combine_kernel(hi_ref, lo_ref, rows_ref, out_ref):
    rows = rows_ref[...]
    total = jnp.dot(hi_ref[...], rows, preferred_element_type=F32)
    total += jnp.dot(lo_ref[...], rows, preferred_element_type=F32)
    out_ref[...] = total.astype(BF16)


def combine(hi, lo, rows):
    count, width = hi.shape[0], rows.shape[1]
    return pl.pallas_call(
        combine_kernel,
        out_shape=jax.ShapeDtypeStruct((count, width), BF16),
        in_specs=[VMEM] * 3,
        out_specs=VMEM,
        cost_estimate=pl.CostEstimate(
            flops=4 * EXPERTS * CAP * count * width, bytes_accessed=2 * (EXPERTS * CAP + count) * width, transcendentals=0
        ),
        compiler_params=pltpu.CompilerParams(vmem_limit_bytes=VMEM_LIMIT),
    )(hi, lo, rows)


def piece(at, gate_up, down):
    _, width, hidden = gate_up.shape
    rows = width // PIECES
    first = lax.dynamic_slice_in_dim(gate_up, at * rows, rows, 1)
    last = [lax.dynamic_slice_in_dim(down, at * rows + n * hidden, hidden, 1) for n in range(rows // hidden)]
    return jnp.concatenate([first, jnp.concatenate(last, axis=0)[None]], axis=0)


def silu_up(gate, up):
    return (gate / (1.0 + jnp.exp(-gate)) * up).astype(BF16)


def experts_kernel(x_ref, arrived_ref, own_gu, own_down, core_gu, core_down, *refs):
    quarters, refs = refs[:10], refs[10:]
    out_hbm, rows_ref, total_ref, gate_up_ref, down_ref, other_ref, out_ref, sem, out_sem, other_sem = refs
    rows_copy = pltpu.make_async_copy(arrived_ref, rows_ref, sem.at[0])
    whole = [
        pltpu.make_async_copy(own_gu, gate_up_ref.at[0], sem.at[1]),
        pltpu.make_async_copy(own_down, down_ref.at[0], sem.at[2]),
        pltpu.make_async_copy(core_gu, gate_up_ref.at[1], sem.at[3]),
        pltpu.make_async_copy(core_down, down_ref.at[1], sem.at[4]),
    ]
    other_copies = [
        pltpu.make_async_copy(q, other_ref.at[i], other_sem.at[i]) for i, q in enumerate(quarters[:6])
    ]
    part = quarters[6].shape[1]
    other_copies += [
        pltpu.make_async_copy(q, other_ref.at[6 + i % 2, :, pl.ds(i // 2 * part, part)], other_sem.at[6 + i])
        for i, q in enumerate(quarters[6:])
    ]
    rows_copy.start()
    for c in whole:
        c.start()
    for c in other_copies:
        c.start()
    rows_copy.wait()
    for s in range(2):
        whole[2 * s].wait()
        rows = rows_ref[...]
        gate = jnp.dot(rows, gate_up_ref[s, 0], preferred_element_type=F32)
        up = jnp.dot(rows, gate_up_ref[s, 1], preferred_element_type=F32)
        hidden = silu_up(gate, up)
        whole[2 * s + 1].wait()
        term = jnp.dot(hidden, down_ref[s], preferred_element_type=F32)
        if s == 0:
            total_ref[...] = term
        else:
            total_ref[...] += term
    for c in other_copies:
        c.wait()
    size = other_ref.shape[2]
    starts = [pl.multiple_of(lax.rem(x_ref[0] + d, PIECES) * size, size) for d in STEPS]
    hidden = []
    for s in range(2):
        gate = up = None
        for k in range(PIECES):
            rows = rows_ref[:, pl.ds(starts[k], size)]
            g = jnp.dot(rows, other_ref[2 * k + s, 0], preferred_element_type=F32)
            u = jnp.dot(rows, other_ref[2 * k + s, 1], preferred_element_type=F32)
            gate, up = (g, u) if gate is None else (gate + g, up + u)
        hidden.append(silu_up(gate, up))
    out_copies = []
    half = size // 2
    for k in range(PIECES):
        for n in range(2):
            at = pl.ds(pl.multiple_of(starts[k] + n * half, half), half)
            term = total_ref[:, at]
            for s in range(2):
                tile = other_ref[2 * k + s, 2, n * half : (n + 1) * half]
                term += jnp.dot(hidden[s], tile, preferred_element_type=F32)
            out_ref[:, at] = term.astype(BF16)
        at = pl.ds(starts[k], size)
        c = pltpu.make_async_copy(out_ref.at[:, at], out_hbm.at[:, at], out_sem.at[k])
        c.start()
        out_copies.append(c)
    for c in out_copies:
        c.wait()


def experts(x, rows, whole, others):
    count, width = rows.shape
    hidden = whole[0].shape[2]
    return pl.pallas_call(
        experts_kernel,
        out_shape=jax.ShapeDtypeStruct((count, width), BF16),
        in_specs=[SMEM] + [HBM] * 15,
        out_specs=HBM,
        scratch_shapes=[
            pltpu.VMEM((count, width), BF16),
            pltpu.VMEM((count, width), F32),
            pltpu.VMEM((2, 2, width, hidden), BF16),
            pltpu.VMEM((2, hidden, width), BF16),
            pltpu.VMEM((2 * PIECES,) + others[0].shape, BF16),
            pltpu.VMEM((count, width), BF16),
            pltpu.SemaphoreType.DMA((5,)),
            pltpu.SemaphoreType.DMA((PIECES,)),
            pltpu.SemaphoreType.DMA((10,)),
        ],
        cost_estimate=pl.CostEstimate(
            flops=24 * count * width * hidden, bytes_accessed=24 * width * hidden, transcendentals=4 * count * hidden
        ),
        compiler_params=pltpu.CompilerParams(vmem_limit_bytes=60 << 20),
    )(x.reshape(1), rows, *whole, *others)


def exchange(rows):
    width = rows.shape[1]
    blocks = rows.reshape(EXPERTS, CAP, width)
    return lax.all_to_all(blocks, ("zh", "yp"), 0, 0, tiled=True).reshape(EXPERTS * CAP, width)


def local(tokens, routes, gates, hot_ids, capacity, gate_up, down):
    x = lax.axis_index("x").astype(jnp.int32)
    near = swap(piece(x, gate_up, down), "yq")
    limits = limits_of(hot_ids, capacity)
    packed = pack(limits, routes.T, tokens)
    hi, lo = row_weights(limits, routes.T, gates.T)
    near, packed = lax.optimization_barrier((near, packed))
    arrived = exchange(packed)
    whole = (gate_up, down, swap(gate_up, "core"), swap(down, "core"))
    before, after = shift(near, 1), shift(near, -1)
    half = near.shape[1] // 2
    quarters = [near, before, after, shift(before[:, :half], 1), shift(after[:, half:], -1)]
    others = [v for q in quarters for v in (q, swap(q, "core"))]
    back = exchange(experts(x, arrived, whole, others))
    return combine(hi, lo, back)


def solution(mesh):
    fine = Mesh(mesh.devices.reshape(SIZES), AXES)
    dp, expert = AXES[:2], AXES[2:]
    in_specs = (
        P(AXES, None),
        P(AXES, None),
        P(AXES, None),
        P(dp),
        P(dp),
        P(None, None, expert),
        P(expert, None),
    )
    return jax.shard_map(local, mesh=fine, in_specs=in_specs, out_specs=P(AXES, None), check_vma=False)
```

```python
import jax
import jax.numpy as jnp
from jax import lax
from jax.experimental import pallas as pl
from jax.experimental.pallas import tpu as pltpu
from jax.sharding import Mesh, PartitionSpec as P

EXPERTS = 8
CAP = 48
F32 = jnp.float32
BF16 = jnp.bfloat16
AXES = ("zl", "x", "zh", "yp", "yq", "core")
SIZES = (4, 4, 2, 4, 2, 2)
VMEM = pl.BlockSpec(memory_space=pltpu.VMEM)
SMEM = pl.BlockSpec(memory_space=pltpu.SMEM)
HBM = pl.BlockSpec(memory_space=pl.ANY)
PIECES = 4
STEPS = (0, 3, 1, 2)
VMEM_LIMIT = 32 << 20


def swap(value, axis):
    return lax.ppermute(value, axis, [(0, 1), (1, 0)])


def shift(value, by):
    return lax.ppermute(value, "x", [(i, (i + by) % 4) for i in range(4)])


def limits_of(hot_ids, capacity):
    e = jnp.arange(EXPERTS, dtype=jnp.int32)
    hot = jnp.logical_or(e == hot_ids[0], e == hot_ids[1])
    return jnp.where(hot, CAP, capacity)


def chosen_rows(limits_ref, routes_ref):
    rows = EXPERTS * CAP
    tokens = routes_ref.shape[1]
    row = lax.broadcasted_iota(jnp.int32, (rows, 1), 0)
    expert = lax.div(row, CAP)
    limit = jnp.zeros((rows, 1), jnp.int32)
    for j in range(EXPERTS):
        limit = jnp.where(expert == j, limits_ref[j], limit)
    first = routes_ref[0:1, :] == expert
    second = routes_ref[1:2, :] == expert
    named = jnp.logical_or(first, second)
    earlier = lax.broadcasted_iota(jnp.int32, (tokens, tokens), 0) < lax.broadcasted_iota(
        jnp.int32, (tokens, tokens), 1
    )
    rank = jnp.dot(
        jnp.where(named, 1.0, 0.0).astype(BF16),
        jnp.where(earlier, 1.0, 0.0).astype(BF16),
        preferred_element_type=F32,
    ).astype(jnp.int32)
    kept = jnp.logical_and(named, rank < limit)
    return jnp.logical_and(kept, rank == lax.rem(row, CAP)), first


def pack_kernel(limits_ref, routes_ref, tokens_ref, packed_ref):
    chosen, _ = chosen_rows(limits_ref, routes_ref)
    place = jnp.where(chosen, 1.0, 0.0).astype(BF16)
    packed_ref[...] = jnp.dot(place, tokens_ref[...], preferred_element_type=F32).astype(BF16)


def pack(limits, routes, tokens):
    count, width = tokens.shape
    return pl.pallas_call(
        pack_kernel,
        out_shape=jax.ShapeDtypeStruct((EXPERTS * CAP, width), BF16),
        in_specs=[SMEM, VMEM, VMEM],
        out_specs=VMEM,
        cost_estimate=pl.CostEstimate(
            flops=2 * EXPERTS * CAP * count * width, bytes_accessed=2 * (EXPERTS * CAP + count) * width, transcendentals=0
        ),
        compiler_params=pltpu.CompilerParams(vmem_limit_bytes=VMEM_LIMIT),
    )(limits, routes, tokens)


def weights_kernel(limits_ref, routes_ref, gates_ref, hi_ref, lo_ref):
    chosen, first = chosen_rows(limits_ref, routes_ref)
    weight = jnp.where(first, gates_ref[0:1, :], gates_ref[1:2, :])
    weight = jnp.where(chosen, weight, 0.0).T
    hi = weight.astype(BF16)
    hi_ref[...] = hi
    lo_ref[...] = (weight - hi.astype(F32)).astype(BF16)


def row_weights(limits, routes, gates):
    shape = jax.ShapeDtypeStruct((routes.shape[1], EXPERTS * CAP), BF16)
    return pl.pallas_call(
        weights_kernel,
        out_shape=[shape, shape],
        in_specs=[SMEM, VMEM, VMEM],
        out_specs=[VMEM, VMEM],
        cost_estimate=pl.CostEstimate(flops=2 * 384 * 128 * 128, bytes_accessed=400000, transcendentals=0),
        compiler_params=pltpu.CompilerParams(vmem_limit_bytes=VMEM_LIMIT),
    )(limits, routes, gates)


def combine_kernel(hi_ref, lo_ref, rows_ref, out_ref):
    rows = rows_ref[...]
    total = jnp.dot(hi_ref[...], rows, preferred_element_type=F32)
    total += jnp.dot(lo_ref[...], rows, preferred_element_type=F32)
    out_ref[...] = total.astype(BF16)


def combine(hi, lo, rows):
    count, width = hi.shape[0], rows.shape[1]
    return pl.pallas_call(
        combine_kernel,
        out_shape=jax.ShapeDtypeStruct((count, width), BF16),
        in_specs=[VMEM] * 3,
        out_specs=VMEM,
        cost_estimate=pl.CostEstimate(
            flops=4 * EXPERTS * CAP * count * width, bytes_accessed=2 * (EXPERTS * CAP + count) * width, transcendentals=0
        ),
        compiler_params=pltpu.CompilerParams(vmem_limit_bytes=VMEM_LIMIT),
    )(hi, lo, rows)


def piece(at, gate_up, down):
    _, width, hidden = gate_up.shape
    rows = width // PIECES
    first = lax.dynamic_slice_in_dim(gate_up, at * rows, rows, 1)
    last = [lax.dynamic_slice_in_dim(down, at * rows + n * hidden, hidden, 1) for n in range(rows // hidden)]
    return jnp.concatenate([first, jnp.concatenate(last, axis=0)[None]], axis=0)


def silu_up(gate, up):
    return (gate / (1.0 + jnp.exp(-gate)) * up).astype(BF16)


def experts_kernel(x_ref, arrived_ref, own_gu, own_down, core_gu, core_down, *refs):
    quarters, refs = refs[:10], refs[10:]
    out_hbm, rows_ref, gate_up_ref, down_ref, other_ref, out_ref, sem, out_sem, other_sem = refs
    rows_copy = pltpu.make_async_copy(arrived_ref, rows_ref, sem.at[0])
    whole = [
        pltpu.make_async_copy(own_gu, gate_up_ref.at[0], sem.at[1]),
        pltpu.make_async_copy(own_down, down_ref.at[0], sem.at[2]),
        pltpu.make_async_copy(core_gu, gate_up_ref.at[1], sem.at[3]),
        pltpu.make_async_copy(core_down, down_ref.at[1], sem.at[4]),
    ]
    other_copies = [
        pltpu.make_async_copy(q, other_ref.at[i], other_sem.at[i]) for i, q in enumerate(quarters[:6])
    ]
    part = quarters[6].shape[1]
    other_copies += [
        pltpu.make_async_copy(q, other_ref.at[6 + i % 2, :, pl.ds(i // 2 * part, part)], other_sem.at[6 + i])
        for i, q in enumerate(quarters[6:])
    ]
    rows_copy.start()
    whole[0].start()
    rows_copy.wait()
    whole[2].start()
    hidden = []
    for s in range(2):
        whole[2 * s].wait()
        for c in other_copies if s == 0 else (whole[1], whole[3]):
            c.start()
        rows = rows_ref[...]
        gate = jnp.dot(rows, gate_up_ref[s, 0], preferred_element_type=F32)
        up = jnp.dot(rows, gate_up_ref[s, 1], preferred_element_type=F32)
        hidden.append(silu_up(gate, up))
    for c in other_copies:
        c.wait()
    size = other_ref.shape[2]
    half = size // 2
    starts = [pl.multiple_of(lax.rem(x_ref[0] + d, PIECES) * size, size) for d in STEPS]
    for s in range(2):
        gate = up = None
        for k in range(PIECES):
            rows = rows_ref[:, pl.ds(starts[k], size)]
            g = jnp.dot(rows, other_ref[2 * k + s, 0], preferred_element_type=F32)
            u = jnp.dot(rows, other_ref[2 * k + s, 1], preferred_element_type=F32)
            gate, up = (g, u) if gate is None else (gate + g, up + u)
        hidden.append(silu_up(gate, up))
    for s in range(2):
        whole[2 * s + 1].wait()
    out_copies = []
    for k in range(PIECES):
        for n in range(2):
            at = pl.ds(pl.multiple_of(starts[k] + n * half, half), half)
            tiles = [down_ref[s, :, at] for s in range(2)]
            tiles += [other_ref[2 * k + s, 2, n * half : (n + 1) * half] for s in range(2)]
            total = None
            for h, tile in zip(hidden, tiles):
                term = jnp.dot(h, tile, preferred_element_type=F32)
                total = term if total is None else total + term
            out_ref[:, at] = total.astype(BF16)
        at = pl.ds(starts[k], size)
        c = pltpu.make_async_copy(out_ref.at[:, at], out_hbm.at[:, at], out_sem.at[k])
        c.start()
        out_copies.append(c)
    for c in out_copies:
        c.wait()


def experts(x, rows, whole, others):
    count, width = rows.shape
    hidden = whole[0].shape[2]
    return pl.pallas_call(
        experts_kernel,
        out_shape=jax.ShapeDtypeStruct((count, width), BF16),
        in_specs=[SMEM] + [HBM] * 15,
        out_specs=HBM,
        scratch_shapes=[
            pltpu.VMEM((count, width), BF16),
            pltpu.VMEM((2, 2, width, hidden), BF16),
            pltpu.VMEM((2, hidden, width), BF16),
            pltpu.VMEM((2 * PIECES,) + others[0].shape, BF16),
            pltpu.VMEM((count, width), BF16),
            pltpu.SemaphoreType.DMA((5,)),
            pltpu.SemaphoreType.DMA((PIECES,)),
            pltpu.SemaphoreType.DMA((10,)),
        ],
        cost_estimate=pl.CostEstimate(
            flops=24 * count * width * hidden, bytes_accessed=24 * width * hidden, transcendentals=4 * count * hidden
        ),
        compiler_params=pltpu.CompilerParams(vmem_limit_bytes=60 << 20),
    )(x.reshape(1), rows, *whole, *others)


def exchange(rows):
    width = rows.shape[1]
    blocks = rows.reshape(EXPERTS, CAP, width)
    return lax.all_to_all(blocks, ("zh", "yp"), 0, 0, tiled=True).reshape(EXPERTS * CAP, width)


def local(tokens, routes, gates, hot_ids, capacity, gate_up, down):
    x = lax.axis_index("x").astype(jnp.int32)
    near = swap(piece(x, gate_up, down), "yq")
    limits = limits_of(hot_ids, capacity)
    packed = pack(limits, routes.T, tokens)
    hi, lo = row_weights(limits, routes.T, gates.T)
    near, packed = lax.optimization_barrier((near, packed))
    arrived = exchange(packed)
    whole = (gate_up, down, swap(gate_up, "core"), swap(down, "core"))
    before, after = shift(near, 1), shift(near, -1)
    half = near.shape[1] // 2
    quarters = [near, before, after, shift(before[:, :half], 1), shift(after[:, half:], -1)]
    others = [v for q in quarters for v in (q, swap(q, "core"))]
    back = exchange(experts(x, arrived, whole, others))
    return combine(hi, lo, back)


def solution(mesh):
    fine = Mesh(mesh.devices.reshape(SIZES), AXES)
    dp, expert = AXES[:2], AXES[2:]
    in_specs = (
        P(AXES, None),
        P(AXES, None),
        P(AXES, None),
        P(dp),
        P(dp),
        P(None, None, expert),
        P(expert, None),
    )
    return jax.shard_map(local, mesh=fine, in_specs=in_specs, out_specs=P(AXES, None), check_vma=False)
```
